32 devices in a mesh: fsdp: 32 (over z, y, x, core).
Axes of the slice: x: 2, y: 2, z: 4, core: 2. Of those that a mesh axis runs over, the one named last changes fastest.
Arguments:
- tokens: bfloat16 [32, 512, 1536], P('fsdp'), may hold values from -6 to 6
- cotangent: bfloat16 [32, 512, 1536], P('fsdp'), may hold values from -6 to 6
- lengths: int32 [32], P('fsdp'), may hold values from 1 to 512, as said below
- weights_in: bfloat16 [1536, 6448], P('fsdp'), may hold values from -0.15625 to 0.15625
- weights_out: bfloat16 [3072, 1536], P('fsdp'), may hold values from -0.109375 to 0.109375
- norm_gain: bfloat16 [1536], P('fsdp'), may hold values from 0.5 to 1.5
- inner_gain: bfloat16 [3072], P('fsdp'), may hold values from 0.5 to 1.5
- kernel_weight: float32 [4, 3328], replicated, may hold values from -3 to 3
- kernel_bias: float32 [3328], replicated, may hold values from -3 to 3
- step_bias: float32 [48], replicated, may hold values from -6 to -2
- log_rates: float32 [48], replicated, may hold values from -1 to 2.5
- skip_gain: float32 [48], replicated, may hold values from 0.5 to 1.5
Outputs:
- output: float32 [32, 512, 1536], P('fsdp')
- grad_tokens: float32 [32, 512, 1536], P('fsdp')
- grad_weights_in: float32 [1536, 6448], P('fsdp')
- grad_weights_out: float32 [3072, 1536], P('fsdp')
- grad_norm_gain: float32 [1536], P('fsdp')
- grad_inner_gain: float32 [3072], P('fsdp')
- grad_kernel_weight: float32 [4, 3328], replicated
- grad_kernel_bias: float32 [3328], replicated
- grad_step_bias: float32 [48], replicated
- grad_log_rates: float32 [48], replicated
- grad_skip_gain: float32 [48], replicated
The draws below stay inside these ranges and needn't reach their ends.
Inputs may be any that keep to these rules, and one draw needn't show every extreme that they name: `lengths`: every slot has 1 to 512 live positions and some slot has exactly 512.
All inputs are finite; a program needn't handle non-finite values.
Results may differ from the reference program's by a relative error of at most 0.007.
Values may be sent and summed in bfloat16 or wider, within the bound.
No kernel may reach another device: no remote copies, remote signals or barrier semaphores. Data moves between devices by JAX's collectives and lax.ppermute only.
A program may use at most 320 MiB of HBM per device.

```python
import jax
import jax.numpy as jnp
from jax import lax

D = 1536
HEADS = 48
HDIM = 64
NST = 128
KCONV = 4
GROUP = 256
LEN = 512
DI = 3072
CONVC = 3328
PROJ = 6448
SEQS = 32


def draw_lengths(key, part):
    values = jax.random.randint(key, (SEQS,), 1, LEN + 1)
    chosen = jax.random.randint(jax.random.fold_in(key, 7), (), 0, SEQS)
    return jnp.where(jnp.arange(SEQS) == chosen, LEN, values).astype(jnp.int32)


def steps_of(key, extent, split, smallest, high):
    def one(axis_at, blocks):
        steps = jax.random.uniform(jax.random.fold_in(jax.random.fold_in(key, 6), axis_at), (blocks,), jnp.float32, smallest / len(split), high / len(split))
        return jnp.repeat(jnp.exp(steps), extent[axis_at] // blocks).reshape((-1,) + (1,) * (len(extent) - axis_at - 1))

    level = one(*split[0])
    for cut in split[1:]:
        level = level * one(*cut)
    return level


def scatter_about(own_key, shape, scale, limit, split=(), dtype=jnp.bfloat16):
    level = steps_of(own_key, shape, split, -0.22, 0.18) if split else 1.0
    values = jax.random.normal(own_key, shape, jnp.float32) * scale * level
    return jnp.minimum(jnp.maximum(values, -limit), limit).astype(dtype)


def setup_inputs(seed: int = 0) -> dict:
    streams_of = jax.random.split(jax.random.key(seed), 13)
    return {
        "tokens": scatter_about(streams_of[0], (SEQS, LEN, D), 1.0, 6.0, ((0, 32),)),
        "cotangent": scatter_about(streams_of[1], (SEQS, LEN, D), 1.0, 6.0, ((0, 32),)),
        "lengths": draw_lengths(jax.random.fold_in(streams_of[12], 71), 0),
        "weights_in": scatter_about(streams_of[3], (D, PROJ), D ** -0.5, 0.15625, ((0, 32),)),
        "weights_out": scatter_about(streams_of[4], (DI, D), DI ** -0.5, 0.109375, ((0, 32),)),
        "norm_gain": jnp.clip(1.0 + 0.1 * jax.random.normal(streams_of[5], (D,), jnp.float32), 0.5, 1.5).astype(jnp.bfloat16),
        "inner_gain": jnp.clip(1.0 + 0.1 * jax.random.normal(streams_of[6], (DI,), jnp.float32), 0.5, 1.5).astype(jnp.bfloat16),
        "kernel_weight": scatter_about(streams_of[7], (KCONV, CONVC), KCONV ** -0.5, 3.0, (), jnp.float32),
        "kernel_bias": scatter_about(streams_of[8], (CONVC,), 0.5, 3.0, (), jnp.float32),
        "step_bias": jnp.clip(jax.random.uniform(streams_of[9], (HEADS,), jnp.float32, -6.0, -2.0), -6.0, -2.0),
        "log_rates": jnp.clip(jax.random.uniform(streams_of[10], (HEADS,), jnp.float32, -1.0, 2.5), -1.0, 2.5),
        "skip_gain": jnp.clip(jax.random.uniform(streams_of[11], (HEADS,), jnp.float32, 0.5, 1.5), 0.5, 1.5),
    }


EPSILON = 1e-05
HIGHEST = lax.Precision.HIGHEST

def rms_scale(values, gain):
    return values * lax.rsqrt(lax.optimization_barrier(jnp.mean(values * values, axis=-1, keepdims=True)) + EPSILON) * gain

def state_space(inputs_x, step_size, decay_rates, in_state, out_state):
    length = inputs_x.shape[0]
    blocks = length // GROUP
    group_x = inputs_x.reshape(blocks, GROUP, HEADS, HDIM)
    group_step = step_size.reshape(blocks, GROUP, HEADS)
    group_in = in_state.reshape(blocks, GROUP, NST)
    group_out = out_state.reshape(blocks, GROUP, NST)
    cumulative = jnp.cumsum(group_step * decay_rates, axis=1).transpose(0, 2, 1)
    position = jnp.arange(GROUP)
    causal = position[:, None] >= position[None, :]
    spread = cumulative[:, :, :, None] - cumulative[:, :, None, :]
    decays = jnp.where(causal, jnp.exp(jnp.where(causal, spread, 0.0)), 0.0)
    scores = jnp.einsum('cin,cjn->cij', group_out, group_in, precision=HIGHEST)
    weighted_x = group_x * group_step[..., None]
    inner_part = jnp.einsum('cij,chij,cjhp->cihp', scores, decays, weighted_x, precision=HIGHEST)
    to_end = jnp.exp(cumulative[:, :, -1:] - cumulative)
    states = jnp.einsum('chj,cjn,cjhp->chpn', to_end, group_in, weighted_x, precision=HIGHEST)
    carry_decay = jnp.exp(cumulative[:, :, -1])

    def advance(carried, members):
        decay_now, state_now = members
        return (decay_now[:, None, None] * carried + state_now, carried)
    initial = jnp.zeros((HEADS, HDIM, NST), jnp.float32)
    final_state, entering = lax.scan(advance, initial, (carry_decay, states))
    outer_part = jnp.einsum('cin,chpn,chi->cihp', group_out, entering, jnp.exp(cumulative), precision=HIGHEST)
    return (inner_part + outer_part).reshape(length, HEADS, HDIM)

def mixer(projected, kernel_weight, kernel_bias, step_bias, log_rates, skip_gain, gain_inner):
    length = projected.shape[0]
    gate_z = projected[:, :DI]
    conv_input = projected[:, DI:DI + CONVC]
    step_raw = projected[:, DI + CONVC:]
    padded = jnp.pad(conv_input, ((KCONV - 1, 0), (0, 0)))
    convolved = kernel_bias + sum((kernel_weight[offset] * padded[offset:offset + length] for offset in range(KCONV)))
    activated = jax.nn.silu(convolved)
    inputs_x = activated[:, :DI].reshape(length, HEADS, HDIM)
    in_state = activated[:, DI:DI + NST]
    out_state = activated[:, DI + NST:]
    step_size = jax.nn.softplus(step_raw + step_bias)
    decay_rates = -jnp.exp(log_rates)
    mixed = state_space(inputs_x, step_size, decay_rates, in_state, out_state) + skip_gain[None, :, None] * inputs_x
    gated = mixed.reshape(length, DI) * jax.nn.silu(gate_z)
    return rms_scale(gated, gain_inner)

def reference(tokens, cotangent, lengths, weights_in, weights_out, norm_gain, inner_gain, kernel_weight, kernel_bias, step_bias, log_rates, skip_gain):
    gain_outer = norm_gain.astype(jnp.float32)
    gain_inner = inner_gain.astype(jnp.float32)

    def one_sequence(totals, members):
        tokens_seq, cotangent_seq, length_seq = members
        residual = tokens_seq.astype(jnp.float32)
        normed, pull_norm = jax.vjp(rms_scale, residual, gain_outer)
        normed_b = normed.astype(jnp.bfloat16)
        projected = jnp.dot(normed_b, weights_in, preferred_element_type=jnp.float32)
        gated, pull_mix = jax.vjp(mixer, projected, kernel_weight, kernel_bias, step_bias, log_rates, skip_gain, gain_inner)
        gated_b = gated.astype(jnp.bfloat16)
        live = jnp.arange(LEN) < length_seq
        full_out = residual + jnp.dot(gated_b, weights_out, preferred_element_type=jnp.float32)
        output_seq = jnp.where(live[:, None], full_out, jnp.zeros_like(full_out))
        d_out = jnp.where(live[:, None], cotangent_seq, jnp.zeros_like(cotangent_seq))
        grad_out_w = jnp.dot(gated_b.T, d_out, preferred_element_type=jnp.float32)
        d_gated = jnp.dot(d_out, weights_out.T, preferred_element_type=jnp.float32)
        mix_grads = pull_mix(d_gated)
        d_projected = mix_grads[0].astype(jnp.bfloat16)
        grad_in_w = jnp.dot(normed_b.T, d_projected, preferred_element_type=jnp.float32)
        d_normed = jnp.dot(d_projected, weights_in.T, preferred_element_type=jnp.float32)
        d_residual, d_gain = pull_norm(d_normed)
        grad_seq = d_out.astype(jnp.float32) + d_residual
        updates = (grad_in_w, grad_out_w, d_gain, mix_grads[6], mix_grads[1], mix_grads[2], mix_grads[3], mix_grads[4], mix_grads[5])
        totals = tuple((total + update for total, update in zip(totals, updates)))
        return (totals, (output_seq, grad_seq))
    initial = (jnp.zeros((D, PROJ), jnp.float32), jnp.zeros((DI, D), jnp.float32), jnp.zeros((D,), jnp.float32), jnp.zeros((DI,), jnp.float32), jnp.zeros((KCONV, CONVC), jnp.float32), jnp.zeros((CONVC,), jnp.float32), jnp.zeros((HEADS,), jnp.float32), jnp.zeros((HEADS,), jnp.float32), jnp.zeros((HEADS,), jnp.float32))
    totals, (output, grad_tokens) = lax.scan(one_sequence, initial, (tokens, cotangent, lengths))
    return (output, grad_tokens, totals[0], totals[1], totals[2], totals[3], totals[4], totals[5], totals[6], totals[7], totals[8])
```

```python
import functools

import jax
import jax.numpy as jnp
from jax import lax
from jax.experimental import pallas as pl
from jax.experimental.pallas import tpu as pltpu
from jax.sharding import PartitionSpec as P

HEADS = 48
HDIM = 64
NST = 128
KCONV = 4
GROUP = 256
DI = 3072
CONVC = 3328
EPSILON = 1e-05

TILE_HEADS = 4
TILE = TILE_HEADS * HDIM
LANES = 128
BCW = 3 * LANES
NPART = 4
F32 = jnp.float32
BF16 = jnp.bfloat16
HEAD_CHUNKS = ((0, 12), (12, 48))


def dot(a, b):
    return lax.dot_general(a, b, (((1,), (0,)), ((), ())), preferred_element_type=F32)


def dot_nt(a, b):
    return lax.dot_general(a, b, (((1,), (1,)), ((), ())), preferred_element_type=F32)


def dot_tn(a, b):
    return lax.dot_general(a, b, (((0,), (0,)), ((), ())), preferred_element_type=F32)


def split2(v):
    hi = v.astype(BF16)
    return hi, (v - hi.astype(F32)).astype(BF16)


def split3(v):
    hi = v.astype(BF16)
    rest = v - hi.astype(F32)
    mid = rest.astype(BF16)
    return hi, mid, (rest - mid.astype(F32)).astype(BF16)


def iota(shape, axis):
    return lax.broadcasted_iota(jnp.int32, shape, axis)


def delayed(v, by):
    if by == 0:
        return v
    return jnp.where(iota(v.shape, 0) >= by, pltpu.roll(v, by, 0), 0.0)


def advanced(v, by):
    if by == 0:
        return v
    rows = v.shape[0]
    return jnp.where(iota(v.shape, 0) < rows - by, pltpu.roll(v, rows - by, 0), 0.0)


def convolve(conv_in, taps, bias):
    total = bias + taps[KCONV - 1 : KCONV] * conv_in
    for back in range(1, KCONV):
        total += taps[KCONV - 1 - back : KCONV - back] * delayed(conv_in, back)
    return total


def convolve_back(d_act, conv_in, taps, bias):
    pre = convolve(conv_in, taps, bias)
    sig = jax.nn.sigmoid(pre)
    d_pre = d_act * (sig * (1.0 + pre * (1.0 - sig)))
    d_in = taps[KCONV - 1 : KCONV] * d_pre
    d_taps = [None] * KCONV
    d_taps[KCONV - 1] = jnp.sum(d_pre * conv_in, axis=0, keepdims=True)
    for back in range(1, KCONV):
        ahead = advanced(d_pre, back)
        d_in += taps[KCONV - 1 - back : KCONV - back] * ahead
        d_taps[KCONV - 1 - back] = jnp.sum(ahead * conv_in, axis=0, keepdims=True)
    return d_in, d_taps, jnp.sum(d_pre, axis=0, keepdims=True)


def head_columns(first):
    return lambda v: [v[:, h : h + 1] for h in range(TILE_HEADS)]


def spread(columns):
    rows = columns[0].shape[0]
    lane = iota((rows, TILE), 1) // HDIM
    out = jnp.broadcast_to(columns[0], (rows, TILE))
    for h in range(1, TILE_HEADS):
        out = jnp.where(lane == h, columns[h], out)
    return out


def tile_heads(v, first_head):
    moved = pltpu.roll(v, LANES - first_head, 1)
    return [moved[:, h : h + 1] for h in range(TILE_HEADS)]


def bc_kernel(length, normed, w0, w1, w2, w3, taps, bias, step_bias, log_rates,
              ci_out, b_out, c_out, bt_out, raw_out, step_out, cum_out, cumt_out, s_out, st_out):
    weights = jnp.concatenate([w0[...], w1[...], w2[...], w3[...]], axis=0)
    proj = dot(normed[...], weights)
    conv_in = proj[:, : 2 * NST]
    ci_out[...] = conv_in
    pre = convolve(conv_in, taps[...], bias[...])
    act = pre * jax.nn.sigmoid(pre)
    b_act = act[:, :NST].astype(BF16)
    c_act = act[:, NST:].astype(BF16)
    b_out[...] = b_act
    c_out[...] = c_act
    bt_out[...] = act[:, :NST].T.astype(BF16)
    raw = proj[:, 2 * NST :] + step_bias[...]
    live = iota(raw.shape, 1) < HEADS
    raw_out[...] = raw
    step = jnp.where(live, jnp.maximum(raw, 0.0) + jnp.log1p(jnp.exp(-jnp.abs(raw))), 0.0)
    step_out[...] = step
    decay = step * -jnp.exp(log_rates[...])
    lower = (iota((GROUP, GROUP), 0) >= iota((GROUP, GROUP), 1)).astype(BF16)
    for blk in range(length // GROUP):
        rows = slice(blk * GROUP, (blk + 1) * GROUP)
        total = sum(dot(lower, piece) for piece in split3(decay[rows]))
        cum_out[rows, :] = total
        cumt_out[:, rows] = total.T
        b_hi, b_lo = split2(act[rows, :NST])
        c_hi, c_lo = split2(act[rows, NST:])
        s_out[blk] = dot_nt(c_hi, b_hi) + dot_nt(c_hi, b_lo) + dot_nt(c_lo, b_hi)
        st_out[blk] = dot_nt(b_hi, c_hi) + dot_nt(b_lo, c_hi) + dot_nt(b_hi, c_lo)


def scan_kernel(length, head0, normed, w0, w1, w2, w3, taps, bias, skip, step_ref, cum_ref, cumt_ref, s_ref, c_ref, bt_ref,
                ci_out, y_out, state_out):
    first = head0 + pl.program_id(0) * TILE_HEADS
    weights = jnp.concatenate([w0[...], w1[...], w2[...], w3[...]], axis=0)
    conv_in = dot(normed[...], weights)
    ci_out[...] = conv_in
    pre = convolve(conv_in, taps[...], bias[...])
    x = pre * jax.nn.sigmoid(pre)
    steps = spread(tile_heads(step_ref[...], first))
    wx = x * steps
    wxb = wx.astype(BF16)
    cum_cols = tile_heads(cum_ref[...], first)
    cums = spread(cum_cols)
    lane_head = iota((GROUP, TILE), 1) // HDIM
    hide = jnp.where(iota((GROUP, GROUP), 0) >= iota((GROUP, GROUP), 1), 0.0, -1e30)
    state = None
    blocks = length // GROUP
    for blk in range(blocks):
        rows = slice(blk * GROUP, (blk + 1) * GROUP)
        wx_blk = wxb[rows]
        scores = s_ref[blk]
        lefts, rights = [], []
        for h in range(TILE_HEADS):
            row = cumt_ref[pl.ds(first + h, 1), rows]
            decays = jnp.exp((cum_cols[h][rows] - row) + hide)
            lefts.append((scores * decays).astype(BF16))
            rights.append(jnp.where(lane_head == h, wx_blk, jnp.zeros_like(wx_blk)))
        y = dot(jnp.concatenate(lefts, axis=1), jnp.concatenate(rights, axis=0))
        cum_blk = cums[rows]
        if state is not None:
            y += dot(c_ref[rows, :], state.astype(BF16)) * jnp.exp(cum_blk)
        y_out[rows, :] = y + skip[...] * x[rows]
        if blk + 1 < blocks:
            last = cum_blk[GROUP - 1 : GROUP]
            kept = dot(bt_ref[:, rows], (jnp.exp(last - cum_blk) * wx[rows]).astype(BF16))
            state = kept if state is None else jnp.exp(last) * state + kept
            state_out[blk] = state


def gate_kernel(normed, w0, w1, w2, w3, y_ref, z_out, g_out, rms_out):
    step = pl.program_id(0)
    weights = jnp.concatenate([w0[...], w1[...], w2[...], w3[...]], axis=0)
    z = dot(normed[...], weights)
    z_out[...] = z
    g = y_ref[...] * (z * jax.nn.sigmoid(z))
    g_out[...] = g

    @pl.when(step == 0)
    def _():
        rms_out[...] = jnp.zeros_like(rms_out)

    rms_out[...] += jnp.sum(g * g, axis=1, keepdims=True)

    @pl.when(step == pl.num_programs(0) - 1)
    def _():
        rms_out[...] = lax.rsqrt(rms_out[...] * (1.0 / DI) + EPSILON)


def out_kernel(slots, table, g_ref, rms_ref, gain_ref, d_out_ref, residual_ref, live_ref, w0, w1, w2, w3,
               out_ref, dgated_ref, dot_ref, dgain_ref, gw0, gw1, gw2, gw3, wv, gwv, sem_in, sem_out):
    step = pl.program_id(0)
    last = pl.num_programs(0) - 1
    width = g_ref.shape[1]
    block = wv.shape[0] // slots
    per = slots // NPART
    sources = (w0, w1, w2, w3)
    targets = (gw0, gw1, gw2, gw3)

    def at(ref, slot):
        return ref.at[pl.ds(pl.multiple_of(table[slot] * block, block), block)]

    @pl.when(step == 0)
    def _():
        for slot in range(slots):
            src = sources[slot // per].at[pl.ds((slot % per) * block, block)]
            pltpu.make_async_copy(src, at(wv, slot), sem_in).start()
        pltpu.make_async_copy(wv, wv, sem_in).wait()

    g = g_ref[...] * rms_ref[...]
    scaled = g * gain_ref[...]
    gated = scaled.astype(BF16)
    rows = wv[pl.ds(pl.multiple_of(step * width, width), width), :]
    part = dot(gated, rows)

    @pl.when(step == 0)
    def _():
        out_ref[...] = residual_ref[...] + part
        dot_ref[...] = jnp.zeros_like(dot_ref)

    @pl.when(step > 0)
    def _():
        out_ref[...] += part

    d_out = d_out_ref[...]
    d_gated = dot_nt(d_out, rows)
    dgated_ref[...] = d_gated
    dot_ref[...] += jnp.sum(d_gated * scaled, axis=1, keepdims=True)
    dgain_ref[...] = jnp.sum(d_gated * g, axis=0, keepdims=True)
    gwv[pl.ds(pl.multiple_of(step * width, width), width), :] = dot_tn(gated, d_out).astype(BF16)

    @pl.when(step == last)
    def _():
        out_ref[...] = jnp.where(live_ref[...] > 0.0, out_ref[...], 0.0)
        for slot in range(slots):
            dst = targets[slot // per].at[pl.ds((slot % per) * block, block)]
            pltpu.make_async_copy(at(gwv, slot), dst, sem_out).start()
        pltpu.make_async_copy(gwv, gwv, sem_out).wait()


def weight_grads(normed_t, d_proj, outs):
    quarter = outs[0].shape[0]
    for part in range(NPART):
        outs[part][...] = dot(normed_t[part * quarter : (part + 1) * quarter, :], d_proj).astype(BF16)


def add_input_grads(dn_out, dn_in, d_proj, weights, first):
    quarter = weights[0].shape[0]
    for part in range(NPART):
        cols = slice(part * quarter, (part + 1) * quarter)
        piece = dot_nt(d_proj, weights[part][...])
        if dn_in is None:
            before = jnp.where(first, 0.0, dn_out[:, cols])
        else:
            before = jnp.where(first, dn_in[:, cols], dn_out[:, cols])
        dn_out[:, cols] = before + piece


def gate_back_kernel(normed_t, w0, w1, w2, w3, dgated, g_ref, y_ref, z_ref, rms, dot_ref, gain, dy_out, g0, g1, g2, g3, dn_out):
    step = pl.program_id(0)
    r = rms[...]
    d_hat = dgated[...] * gain[...]
    dg = r * (d_hat - (g_ref[...] * r) * (dot_ref[...] * (1.0 / DI)))
    z = z_ref[...]
    sig = jax.nn.sigmoid(z)
    dy_out[...] = dg * (z * sig)
    dz = (dg * y_ref[...] * (sig * (1.0 + z * (1.0 - sig)))).astype(BF16)
    weight_grads(normed_t, dz, (g0, g1, g2, g3))
    add_input_grads(dn_out, None, dz, (w0, w1, w2, w3), step == 0)


def scan_back_kernel(length, head0, normed_t, w0, w1, w2, w3, dy_ref, y_ref, ci_ref, taps, bias, skip, step_ref, cum_ref, cumt_ref,
                     st_ref, b_ref, c_ref, ct_ref, state_ref, dn_in, dst_in, db_in, dc_in, dcum_in, dstep_in,
                     g0, g1, g2, g3, dskip_out, dtaps_out, dbias_out, dn_out, dst_out, db_out, dc_out, dcum_out, dstep_out):
    pid = pl.program_id(0)
    begin = pid == 0
    first = head0 + pid * TILE_HEADS

    @pl.when(begin)
    def _():
        dst_out[...] = dst_in[...]
        db_out[...] = db_in[...]
        dc_out[...] = dc_in[...]
        dcum_out[...] = dcum_in[...]
        dstep_out[...] = dstep_in[...]

    conv_in = ci_ref[...]
    pre = convolve(conv_in, taps[...], bias[...])
    x = pre * jax.nn.sigmoid(pre)
    dy = dy_ref[...]
    dyb = dy.astype(BF16)
    dskip_out[...] = jnp.sum(dy * x, axis=0, keepdims=True)
    steps = spread(tile_heads(step_ref[...], first))
    wx = x * steps
    wxb = wx.astype(BF16)
    cum_cols = tile_heads(cum_ref[...], first)
    cums = spread(cum_cols)
    y_scan = y_ref[...] - skip[...] * x
    lane_head = iota((GROUP, TILE), 1) // HDIM
    hide = jnp.where(iota((GROUP, GROUP), 1) >= iota((GROUP, GROUP), 0), 0.0, -1e30)
    pick = (iota((TILE, LANES), 1) == first + iota((TILE, LANES), 0) // HDIM).astype(BF16)

    def per_head(v):
        hi, lo = split2(v)
        return dot(hi, pick) + dot(lo, pick)

    blocks = length // GROUP
    d_state = None
    dwx_blocks = [None] * blocks
    for blk in reversed(range(blocks)):
        rows = slice(blk * GROUP, (blk + 1) * GROUP)
        dy_blk, wx_blk, cum_blk = dyb[rows], wxb[rows], cums[rows]
        scores = st_ref[blk]
        lefts, rights = [], []
        d_scores = None
        for h in range(TILE_HEADS):
            row = cumt_ref[pl.ds(first + h, 1), rows]
            decays = jnp.exp((row - cum_cols[h][rows]) + hide)
            lefts.append((scores * decays).astype(BF16))
            rights.append(jnp.where(lane_head == h, dy_blk, jnp.zeros_like(dy_blk)))
            piece = dot_nt(jnp.where(lane_head == h, wx_blk, jnp.zeros_like(wx_blk)), dy_blk) * decays
            d_scores = piece if d_scores is None else d_scores + piece
        dst_out[blk] += d_scores
        dwx = dot(jnp.concatenate(lefts, axis=1), jnp.concatenate(rights, axis=0))
        last = cum_blk[GROUP - 1 : GROUP]
        at_end = None
        if d_state is not None:
            to_end = jnp.exp(last - cum_blk)
            d_state_b = d_state.astype(BF16)
            leaving = to_end * dot(b_ref[rows, :], d_state_b)
            dwx += leaving
            db_out[rows, :] += dot_nt((to_end * wx[rows]).astype(BF16), d_state_b)
            at_end = jnp.sum(wx_blk.astype(F32) * leaving, axis=0, keepdims=True)
            if blk > 0:
                at_end += jnp.exp(last) * jnp.sum(d_state * state_ref[blk - 1], axis=0, keepdims=True)
            at_end = per_head(at_end)
        dwx_blocks[blk] = dwx
        moved = per_head(dy_blk.astype(F32) * y_scan[rows] - wx_blk.astype(F32) * dwx)
        if at_end is not None:
            moved += jnp.where(iota((GROUP, LANES), 0) == GROUP - 1, at_end, 0.0)
        dcum_out[rows, :] += moved
        if blk > 0:
            from_start = jnp.exp(cum_blk)
            scaled = (from_start * dy[rows]).astype(BF16)
            dc_out[rows, :] += dot_nt(scaled, state_ref[blk - 1].astype(BF16))
            fresh = dot(ct_ref[:, rows], scaled)
            d_state = fresh if d_state is None else jnp.exp(last) * d_state + fresh
    dwx = jnp.concatenate(dwx_blocks, axis=0)
    dstep_out[...] += per_head(dwx * x)
    dx = dwx * steps + skip[...] * dy
    d_in, d_taps, d_bias = convolve_back(dx, conv_in, taps[...], bias[...])
    for tap in range(KCONV):
        dtaps_out[tap : tap + 1, :] = d_taps[tap]
    dbias_out[...] = d_bias
    d_proj = d_in.astype(BF16)
    weight_grads(normed_t, d_proj, (g0, g1, g2, g3))
    add_input_grads(dn_out, dn_in, d_proj, (w0, w1, w2, w3), begin)


def bc_back_kernel(length, normed_t, w0, w1, w2, w3, ci_ref, taps, bias, raw_ref, step_ref, log_rates, b_ref, c_ref,
                   dst_ref, db_ref, dc_ref, dcum_ref, dstep_ref, dn_in, residual, gain,
                   g0, g1, g2, g3, dtaps_out, dbias_out, dsb_out, dlr_out, dres_out, dgain_out):
    upper = (iota((GROUP, GROUP), 1) >= iota((GROUP, GROUP), 0)).astype(BF16)
    d_b, d_c, d_decay = [], [], []
    for blk in range(length // GROUP):
        rows = slice(blk * GROUP, (blk + 1) * GROUP)
        d_scores = dst_ref[blk].astype(BF16)
        d_b.append(db_ref[rows, :] + dot(d_scores, c_ref[rows, :]))
        d_c.append(dc_ref[rows, :] + dot_tn(d_scores, b_ref[rows, :]))
        d_decay.append(sum(dot(upper, piece) for piece in split3(dcum_ref[rows, :])))
    d_act = jnp.concatenate([jnp.concatenate(d_b, axis=0), jnp.concatenate(d_c, axis=0)], axis=1)
    d_decay = jnp.concatenate(d_decay, axis=0)
    d_in, d_taps, d_bias = convolve_back(d_act, ci_ref[...], taps[...], bias[...])
    for tap in range(KCONV):
        dtaps_out[tap : tap + 1, :] = d_taps[tap]
    dbias_out[...] = d_bias
    rates = -jnp.exp(log_rates[...])
    live = iota(d_decay.shape, 1) < HEADS
    d_raw = (d_decay * rates + dstep_ref[...]) * jax.nn.sigmoid(raw_ref[...])
    d_raw = jnp.where(live, d_raw, 0.0)
    dsb_out[...] = jnp.sum(d_raw, axis=0, keepdims=True)
    dlr_out[...] = jnp.sum(d_decay * step_ref[...], axis=0, keepdims=True) * rates
    d_proj = jnp.concatenate([d_in, d_raw], axis=1).astype(BF16)
    weight_grads(normed_t, d_proj, (g0, g1, g2, g3))
    pieces = [dot_nt(d_proj, w[...]) for w in (w0, w1, w2, w3)]
    d_normed = dn_in[...] + jnp.concatenate(pieces, axis=1)
    res = residual[...]
    width = res.shape[1]
    r = lax.rsqrt(jnp.sum(res * res, axis=1, keepdims=True) * (1.0 / width) + EPSILON)
    hat = res * r
    dgain_out[...] = jnp.sum(d_normed * hat, axis=0, keepdims=True)
    d_hat = d_normed * gain[...]
    inner = jnp.sum(d_hat * hat, axis=1, keepdims=True) * (1.0 / width)
    dres_out[...] = r * (d_hat - hat * inner)


def shape(dims, dtype=F32):
    return jax.ShapeDtypeStruct(dims, dtype)


def whole(arr):
    dims = arr.shape
    return pl.BlockSpec(dims, lambda i: (0,) * len(dims))


def columns(rows, width, offset=0):
    return pl.BlockSpec((rows, width), lambda i: (0, i + offset))


def call(kernel, grid, in_specs, out_specs, out_shape, args, scratch=(), flops=0, prefetch=0):
    moved = sum(a.size * a.dtype.itemsize for a in args) + sum(s.size * s.dtype.itemsize for s in out_shape)
    return pl.pallas_call(
        kernel,
        grid_spec=pltpu.PrefetchScalarGridSpec(
            num_scalar_prefetch=prefetch, grid=(grid,), in_specs=in_specs, out_specs=out_specs, scratch_shapes=scratch
        ),
        out_shape=out_shape,
        compiler_params=pltpu.CompilerParams(
            dimension_semantics=("arbitrary",), vmem_limit_bytes=60 * 1024 * 1024
        ),
        cost_estimate=pl.CostEstimate(flops=int(flops), bytes_accessed=int(moved), transcendentals=0),
    )(*args)


def project_bc(normed, parts, taps, bias, step_bias, log_rates):
    length, width = normed.shape
    blocks = length // GROUP
    args = (normed, *parts, taps, bias, step_bias, log_rates)
    outs = [
        shape((length, 2 * NST)), shape((length, NST), BF16), shape((length, NST), BF16), shape((NST, length), BF16),
        shape((length, LANES)), shape((length, LANES)), shape((length, LANES)), shape((LANES, length)),
        shape((blocks, GROUP, GROUP)), shape((blocks, GROUP, GROUP)),
    ]
    quarter = width // NPART
    offset = parts[0].shape[1] // BCW - 1
    w_spec = pl.BlockSpec((quarter, BCW), lambda i: (0, offset))
    specs = [whole(normed)] + [w_spec] * NPART + [whole(a) for a in args[1 + NPART :]]
    return call(functools.partial(bc_kernel, length), 1, specs, [whole(o) for o in outs], outs, args,
                flops=2 * length * width * BCW)


def scan_forward(normed, parts, head0, heads, taps, bias, skip, step, cum, cumt, scores, c_act, b_t):
    length, width = normed.shape
    quarter = width // NPART
    tiles = heads // TILE_HEADS
    at = head0 // TILE_HEADS
    cols = heads * HDIM
    blocks = length // GROUP
    args = (normed, *parts, taps, bias, skip, step, cum, cumt, scores, c_act, b_t)
    specs = (
        [whole(normed)] + [columns(quarter, TILE)] * NPART
        + [columns(KCONV, TILE, at), columns(1, TILE, at), columns(1, TILE, at)]
        + [whole(a) for a in args[4 + NPART :]]
    )
    outs = [shape((length, cols)), shape((length, cols)), shape((blocks - 1, NST, cols))]
    out_specs = [columns(length, TILE), columns(length, TILE), pl.BlockSpec((blocks - 1, NST, TILE), lambda i: (0, 0, i))]
    return call(functools.partial(scan_kernel, length, head0), tiles, specs, out_specs, outs, args,
                flops=2 * length * cols * (width + GROUP * 4))


def gate_forward(normed, parts, y):
    length, width = normed.shape
    quarter = width // NPART
    outs = [shape((length, DI)), shape((length, DI)), shape((length, 1))]
    args = (normed, *parts, y)
    specs = [whole(normed)] + [columns(quarter, TILE)] * NPART + [columns(length, TILE)]
    return call(gate_kernel, DI // TILE, specs, [columns(length, TILE), columns(length, TILE), whole(outs[2])], outs, args,
                flops=2 * length * width * DI)


def out_project(table, g, rms, gain, d_out, residual, live, parts):
    length, width = d_out.shape
    slots = table.shape[0]
    args = (table, g, rms, gain, d_out, residual, live, *parts)
    hbm = pl.BlockSpec(memory_space=pl.ANY)

    def fixed(arr):
        dims = arr.shape
        return pl.BlockSpec(dims, lambda i, t: (0,) * len(dims))

    def cols(rows, w):
        return pl.BlockSpec((rows, w), lambda i, t: (0, i))

    specs = [cols(length, TILE), fixed(rms), cols(1, TILE), fixed(d_out), fixed(residual), fixed(live)] + [hbm] * NPART
    outs = [shape((length, width)), shape((length, DI)), shape((length, 1)), shape((1, DI))]
    outs += [shape((DI // NPART, width), BF16)] * NPART
    out_specs = [fixed(outs[0]), cols(length, TILE), fixed(outs[2]), cols(1, TILE)] + [hbm] * NPART
    scratch = [pltpu.VMEM((DI, width), BF16), pltpu.VMEM((DI, width), BF16), pltpu.SemaphoreType.DMA, pltpu.SemaphoreType.DMA]
    return call(functools.partial(out_kernel, slots), DI // TILE, specs, out_specs, outs, args,
                scratch=scratch, flops=6 * length * width * DI, prefetch=1)


def gate_backward(normed_t, parts, dgated, g, y, z, rms, dots, gain):
    width, length = normed_t.shape
    quarter = width // NPART
    args = (normed_t, *parts, dgated, g, y, z, rms, dots, gain)
    tile = columns(length, TILE)
    w_spec = columns(quarter, TILE)
    specs = [whole(normed_t)] + [w_spec] * NPART + [tile] * 4 + [whole(rms), whole(dots), columns(1, TILE)]
    outs = [shape((length, DI))] + [shape((quarter, DI), BF16)] * NPART + [shape((length, width))]
    return call(gate_back_kernel, DI // TILE, specs, [tile] + [w_spec] * NPART + [whole(outs[-1])], outs, args,
                flops=4 * length * width * DI)


def scan_backward(normed_t, parts, head0, heads, dy, y, conv_in, taps, bias, skip, step, cum, cumt, scores_t, b_act, c_act,
                  c_t, state, carried):
    width, length = normed_t.shape
    quarter = width // NPART
    tiles = heads // TILE_HEADS
    at = head0 // TILE_HEADS
    cols = heads * HDIM
    blocks = length // GROUP
    args = (normed_t, *parts, dy, y, conv_in, taps, bias, skip, step, cum, cumt, scores_t, b_act, c_act, c_t, state, *carried)
    w_spec = columns(quarter, TILE)
    local = columns(length, TILE)
    specs = (
        [whole(normed_t)] + [w_spec] * NPART + [columns(length, TILE, at), local, local]
        + [columns(KCONV, TILE, at), columns(1, TILE, at), columns(1, TILE, at)]
        + [whole(a) for a in (step, cum, cumt, scores_t, b_act, c_act, c_t)]
        + [pl.BlockSpec((blocks - 1, NST, TILE), lambda i: (0, 0, i))] + [whole(a) for a in carried]
    )
    outs = [shape((quarter, cols), BF16)] * NPART + [shape((1, cols)), shape((KCONV, cols)), shape((1, cols))]
    outs += [shape(a.shape) for a in carried]
    out_specs = [w_spec] * NPART + [columns(1, TILE), columns(KCONV, TILE), columns(1, TILE)] + [whole(a) for a in carried]
    return call(functools.partial(scan_back_kernel, length, head0), tiles, specs, out_specs, outs, args,
                flops=2 * length * cols * (2 * width + GROUP * 8))


def bc_backward(normed_t, parts, conv_in, taps, bias, raw, step, log_rates, b_act, c_act, dst, db, dc, dcum, dstep, dn, residual, gain):
    width, length = normed_t.shape
    quarter = width // NPART
    args = (normed_t, *parts, conv_in, taps, bias, raw, step, log_rates, b_act, c_act, dst, db, dc, dcum, dstep, dn, residual, gain)
    offset = parts[0].shape[1] // BCW - 1
    w_spec = pl.BlockSpec((quarter, BCW), lambda i: (0, offset))
    specs = [whole(normed_t)] + [w_spec] * NPART + [whole(a) for a in args[1 + NPART :]]
    outs = [shape((quarter, BCW), BF16)] * NPART
    outs += [shape((KCONV, 2 * NST)), shape((1, 2 * NST)), shape((1, LANES)), shape((1, LANES)), shape((length, width)), shape((1, width))]
    return call(functools.partial(bc_back_kernel, length), 1, specs, [whole(o) for o in outs], outs, args,
                flops=4 * length * width * BCW)


class Cube:
    def __init__(self, count):
        bits = count.bit_length() - 1
        assert count == 1 << bits and bits >= 3
        self.count = count
        self.outer = [1 << b for b in reversed(range(3, bits))]

    def swap(self, arr, mask):
        return lax.ppermute(arr, "fsdp", [(i, i ^ mask) for i in range(self.count)])

    def mixed(self, arr, even, odd):
        return lax.ppermute(arr, "fsdp", [(i, i ^ (odd if i & 1 else even)) for i in range(self.count)])

    def slot_owner(self):
        me = lax.axis_index("fsdp")
        slot = jnp.arange(self.count, dtype=jnp.int32)
        inner = len(self.outer)
        owner = jnp.full_like(slot, 0)
        for b, mask in enumerate(self.outer):
            owner = owner ^ (((slot >> b) & 1) * mask)
        near, far, other = (slot >> inner) & 1, (slot >> (inner + 1)) & 1, (slot >> (inner + 2)) & 1
        odd = (me & 1) ^ other
        owner = owner ^ (near * jnp.where(odd == 1, 4, 2)) ^ (far * jnp.where(odd == 1, 2, 4)) ^ other
        return owner ^ me

    def gather(self, shard):
        held = shard
        for mask in self.outer:
            held = jnp.concatenate([held, self.swap(held, mask)], axis=0)
        held = jnp.concatenate([held, self.mixed(held, 2, 4)], axis=0)
        far = self.mixed(held, 4, 2)
        return [held, far, self.swap(held, 1), self.swap(far, 1)]

    def reduce_scatter(self, parts):
        def add(a, b):
            return a.astype(F32) + b.astype(F32)

        far = add(parts[1], self.swap(parts[3], 1)).astype(BF16)
        near = add(parts[0], self.swap(parts[2], 1)).astype(BF16)
        got = self.mixed(far, 4, 2)
        moves = [lambda a: self.mixed(a, 2, 4)] + [functools.partial(self.swap, mask=m) for m in reversed(self.outer)]
        for move in moves:
            half = near.shape[0] // 2
            high = add(near[half:], got[half:]).astype(BF16)
            low = add(near[:half], got[:half]).astype(BF16)
            near, got = low, move(high)
        return add(near, got)

    def all_reduce(self, arr):
        for mask in [1, 2, 4] + self.outer:
            arr = arr + self.swap(arr, mask)
        return arr


def local(tokens, cotangent, lengths, weights_in, weights_out, norm_gain, inner_gain, kernel_weight, kernel_bias,
          step_bias, log_rates, skip_gain, *, count):
    cube = Cube(count)
    seqs, length, width = tokens.shape
    assert seqs == 1
    rows_in, rows_out = weights_in.shape[0], weights_out.shape[0]
    owner = cube.slot_owner()

    extras = jnp.concatenate([norm_gain.reshape(rows_in, 1), inner_gain.reshape(rows_in, DI // width)], axis=1)
    w_z = weights_in[:, :DI]
    w_bc = jnp.concatenate([weights_in[:, 2 * DI :], extras], axis=1)
    w_bc = jnp.pad(w_bc, ((0, 0), (0, BCW - w_bc.shape[1])))
    parts_x = []
    for n, (lo, hi) in enumerate(HEAD_CHUNKS):
        piece = weights_in[:, DI + lo * HDIM : DI + hi * HDIM]
        parts_x.append(cube.gather(jnp.concatenate([piece, w_bc], axis=1) if n == 0 else piece))
    parts_z = cube.gather(w_z)
    parts_out = cube.gather(weights_out)

    at = 2 * NST + HEADS + (HEAD_CHUNKS[0][1] - HEAD_CHUNKS[0][0]) * HDIM
    gains = jnp.concatenate([p[:, at : at + 1 + DI // width] for p in parts_x[0]], axis=0)
    gain_row = gains[:, 0].astype(F32).reshape(1, width)
    inner_row = jnp.zeros((count, rows_out), BF16).at[owner].set(gains[:, 1:].reshape(count, rows_out))
    inner_row = inner_row.astype(F32).reshape(1, DI)

    column = jnp.arange(width, dtype=jnp.int32)
    source = jnp.broadcast_to(owner[:, None] * rows_in, (count, rows_in)) + jnp.arange(rows_in, dtype=jnp.int32)[None]
    order = (column[:, None] == source.reshape(1, width)).astype(BF16)

    seq = tokens.reshape(length, width)
    res_slot = dot(seq, order)
    rms = lax.rsqrt(jnp.mean(res_slot * res_slot, axis=1, keepdims=True) + EPSILON)
    normed = (res_slot * rms * gain_row).astype(BF16)
    normed_t = normed.T

    taps_x, taps_bc = kernel_weight[:, :DI], kernel_weight[:, DI:]
    bias_x, bias_bc = kernel_bias[None, :DI], kernel_bias[None, DI:]
    pad_heads = lambda v: jnp.pad(v, (0, LANES - HEADS)).reshape(1, LANES)
    rates_row = pad_heads(log_rates)
    skip_row = jnp.repeat(skip_gain, HDIM).reshape(1, DI)

    conv_bc, b_act, c_act, b_t, raw, step, cum, cumt, scores, scores_t = project_bc(
        normed, parts_x[0], taps_bc, bias_bc, pad_heads(step_bias), rates_row
    )
    convs, ys, states = [], [], []
    for (lo, hi), parts in zip(HEAD_CHUNKS, parts_x):
        ci, y, st = scan_forward(normed, parts, lo, hi - lo, taps_x, bias_x, skip_row, step, cum, cumt, scores, c_act, b_t)
        convs.append(ci)
        ys.append(y)
        states.append(st)
    y_all = jnp.concatenate(ys, axis=1)
    z, g, inner_rms = gate_forward(normed, parts_z, y_all)

    live = (jnp.arange(length, dtype=jnp.int32)[:, None] < lengths[0]).astype(F32)
    d_out = jnp.where(live > 0.0, cotangent.reshape(length, width), jnp.zeros((), BF16))
    out, dgated, dots, d_inner, *grad_out = out_project(
        owner, g, inner_rms, inner_row, d_out, seq.astype(F32), live, parts_out
    )
    grad_out_w = cube.reduce_scatter(grad_out)

    dy, gz0, gz1, gz2, gz3, dn = gate_backward(normed_t, parts_z, dgated, g, y_all, z, inner_rms, dots, inner_row)
    grad_z = cube.reduce_scatter([gz0, gz1, gz2, gz3])

    blocks = length // GROUP
    carried = (
        dn, jnp.zeros((blocks, GROUP, GROUP), F32), jnp.zeros((length, NST), F32), jnp.zeros((length, NST), F32),
        jnp.zeros((length, LANES), F32), jnp.zeros((length, LANES), F32),
    )
    c_t = c_act.T
    grads_x, d_skip, d_taps, d_bias = [], [], [], []
    for n, (lo, hi) in enumerate(HEAD_CHUNKS):
        g0, g1, g2, g3, dsk, dtp, dbs, *carried = scan_backward(
            normed_t, parts_x[n], lo, hi - lo, dy, ys[n], convs[n], taps_x, bias_x, skip_row, step, cum, cumt, scores_t,
            b_act, c_act, c_t, states[n], carried
        )
        grads_x.append(cube.reduce_scatter([g0, g1, g2, g3]))
        d_skip.append(dsk)
        d_taps.append(dtp)
        d_bias.append(dbs)
    dn, dst, db, dc, dcum, dstep = carried
    g0, g1, g2, g3, dtp, dbs, dsb, dlr, dres, dgain = bc_backward(
        normed_t, parts_x[0], conv_bc, taps_bc, bias_bc, raw, step, rates_row, b_act, c_act, dst, db, dc, dcum, dstep, dn,
        res_slot, gain_row
    )
    grad_bc = cube.reduce_scatter([g0, g1, g2, g3])
    d_taps.append(dtp)
    d_bias.append(dbs)

    hi, lo = split2(dres)
    d_residual = dot_nt(hi, order) + dot_nt(lo, order)
    grad_tokens = d_out.astype(F32) + d_residual

    dgain = jnp.zeros((count, rows_in), F32).at[owner].set(dgain.reshape(count, rows_in))
    small = [
        dgain.reshape(-1), d_inner.reshape(-1), jnp.concatenate(d_taps, axis=1).reshape(-1),
        jnp.concatenate(d_bias, axis=1).reshape(-1), dsb[0, :HEADS], dlr[0, :HEADS],
        jnp.sum(jnp.concatenate(d_skip, axis=1).reshape(HEADS, HDIM), axis=1),
    ]
    flat = jnp.concatenate(small)
    pad = -flat.shape[0] % (8 * LANES)
    flat = cube.all_reduce(jnp.pad(flat, (0, pad)).reshape(-1, LANES)).reshape(-1)
    pieces, start = [], 0
    for item in small:
        pieces.append(flat[start : start + item.shape[0]])
        start += item.shape[0]
    me = lax.axis_index("fsdp")
    grad_norm = lax.dynamic_slice(pieces[0], (me * rows_in,), (rows_in,))
    grad_inner = lax.dynamic_slice(pieces[1], (me * rows_out,), (rows_out,))
    grad_in_w = jnp.concatenate([grad_z, *grads_x, grad_bc[:, : 2 * NST + HEADS]], axis=1)
    return (
        out.reshape(tokens.shape), grad_tokens.reshape(tokens.shape), grad_in_w, grad_out_w, grad_norm, grad_inner,
        pieces[2].reshape(KCONV, CONVC), pieces[3], pieces[4], pieces[5], pieces[6],
    )


def solution(mesh):
    shard, rep = P("fsdp"), P()
    return jax.shard_map(
        functools.partial(local, count=mesh.shape["fsdp"]),
        mesh=mesh,
        in_specs=(shard,) * 7 + (rep,) * 5,
        out_specs=(shard,) * 6 + (rep,) * 5,
        check_vma=False,
    )
```
